32 devices in a mesh: groups: 2 (over y), dp: 4 (over x, core), fsdp: 4 (over z).
Axes of the slice: x: 2, y: 2, z: 4, core: 2. Of those that a mesh axis runs over, the one named last changes fastest.
Arguments:
- facies: int32 [128, 64, 2048], P(('groups', 'dp', 'fsdp')), parts along dimension 0, may hold values from 0 to 3
- prior_draws: bfloat16 [128, 512], P(('groups', 'dp', 'fsdp')), parts along dimension 0, may hold values from -6 to 6
- recon_grad: bfloat16 [128, 512], P(('groups', 'dp', 'fsdp')), parts along dimension 0, may hold values from -0.796875 to 0.796875
- w_embed: bfloat16 [256, 128], replicated, may hold values from -0.75 to 0.75
- w_conv: bfloat16 [1024, 256], replicated, may hold values from -0.1875 to 0.1875
- w_head: bfloat16 [256, 512], replicated, may hold values from -1 to 1
Outputs:
- grad_embed: float32 [512, 128], P(('groups', 'fsdp')), parts along dimension 0
- grad_conv: float32 [2048, 256], P(('groups', 'fsdp')), parts along dimension 0
- grad_head: float32 [512, 512], P(('groups', 'fsdp')), parts along dimension 0
The draws below stay inside these ranges and needn't reach their ends.
There are 2 independent parts, one for each index of `groups`. The reference program is written for one: setup_inputs(seed, part) draws one part's arguments, and reference() takes and returns one part's arrays. A program takes and returns all parts, laid end to end along the dimension named above; an argument that names none is the same for every part. Nothing has to cross between parts.
All inputs are finite; a program needn't handle non-finite values.
Results may differ from the reference program's by a relative error of at most 0.0012.
Values may be sent and summed in bfloat16 or wider, within the bound.
A program may use at most 256 MiB of HBM per device.

```python
import jax
import jax.numpy as jnp
from jax import lax

FACIES = 4
C1 = 128
C2 = 256
LAT = 512
PATCH_X = 64
PATCH_Y = 64
PATCH_Z = 32
SAMP_DEV = 4
SAMPLES = 64


def draw_facies(key, part):
    keys = jax.random.split(key, 8)
    voxel_count = PATCH_X * PATCH_Y * PATCH_Z
    levels = jnp.arange(FACIES, dtype=jnp.int32)
    dominant = jax.random.randint(keys[0], (SAMPLES, 1), 0, FACIES)
    weights = jax.random.randint(keys[1], (SAMPLES, FACIES), 1, 5)
    boost = jax.random.randint(keys[2], (SAMPLES, 1), 6, 40)
    weights = weights + boost * (levels[None, :] == dominant).astype(jnp.int32)
    bounds = jnp.cumsum(weights, axis=1)
    layer_count = max(PATCH_X, PATCH_Y, PATCH_Z) + 8
    picks = jax.random.randint(keys[3], (SAMPLES, layer_count), 0, bounds[:, -1:])
    layer_cat = jnp.sum((picks[:, :, None] >= bounds[:, None, :]).astype(jnp.int32), axis=2)
    orient = jax.random.randint(keys[4], (SAMPLES, 1), 0, 3)
    thick = jax.random.randint(keys[5], (SAMPLES, 1), 1, 7)
    phase = jax.random.randint(keys[6], (SAMPLES, 1), 0, 8)
    voxel = jnp.arange(voxel_count, dtype=jnp.int32)[None, :]
    coord_x = voxel // (PATCH_Y * PATCH_Z)
    coord_y = voxel // PATCH_Z % PATCH_Y
    coord_z = voxel % PATCH_Z
    position = jnp.where(orient == 0, coord_x, jnp.where(orient == 1, coord_y, coord_z))
    layer_id = (position + phase) // thick
    layered = jnp.take_along_axis(layer_cat, layer_id, axis=1)
    rough = jax.random.randint(keys[7], (SAMPLES, voxel_count), 0, 8 * FACIES)
    result = jnp.where(rough < FACIES, rough, layered)
    return result.reshape(SAMPLES, PATCH_X, PATCH_Y * PATCH_Z).astype(jnp.int32)


def level_of(own_key, extent, shards, least, top_value):
    def one(axis_at, parts):
        steps = jax.random.uniform(jax.random.fold_in(jax.random.fold_in(own_key, 6), axis_at), (parts,), jnp.float32, least / len(shards), top_value / len(shards))
        return jnp.repeat(jnp.exp(steps), extent[axis_at] // parts).reshape((-1,) + (1,) * (len(extent) - axis_at - 1))

    level = one(*shards[0])
    for cut in shards[1:]:
        level = level * one(*cut)
    return level


def scatter_about(stream_key, shape, scale, bound, pieces=(), kind=jnp.bfloat16):
    drawn = scale * jax.random.normal(stream_key, shape, jnp.float32)
    if pieces:
        drawn = drawn * level_of(stream_key, shape, pieces, -0.22, 0.18)
    return jnp.clip(drawn, -bound, bound).astype(kind)


def setup_inputs(seed: int = 0, part: int = 0) -> dict:
    arg_keys = jax.random.split(jax.random.key(seed), 7)
    part_splits = jax.random.split(jax.random.fold_in(arg_keys[6], part), 7)
    return {
        "facies": draw_facies(jax.random.fold_in(jax.random.fold_in(arg_keys[6], part), 71), part),
        "prior_draws": scatter_about(part_splits[1], (SAMPLES, LAT), 1.0, 6.0, ((0, 16),)),
        "recon_grad": scatter_about(part_splits[2], (SAMPLES, LAT), 0.1, 0.796875, ((0, 16),)),
        "w_embed": scatter_about(arg_keys[3], (64 * FACIES, C1), 64 ** -0.5, 0.75),
        "w_conv": scatter_about(arg_keys[4], (8 * C1, C2), (8 * C1) ** -0.5, 0.1875),
        "w_head": scatter_about(arg_keys[5], (C2, LAT), (C2 // 8) ** -0.5, 1.0),
    }


def silu_slope(pre_act):
    sigmoid_val = jax.nn.sigmoid(pre_act)
    return sigmoid_val * (1.0 + pre_act * (1.0 - sigmoid_val))


def embed_rows(facies, levels_count):
    samples = facies.shape[0]
    voxels = facies.reshape(samples, PATCH_X // 4, 4, PATCH_Y // 4, 4, PATCH_Z // 4, 4)
    voxels = voxels.transpose(0, 1, 3, 5, 2, 4, 6).reshape(-1, 64)
    levels = jnp.arange(levels_count, dtype=jnp.int32)
    one_hot = (voxels[:, :, None] == levels[None, None, :]).astype(jnp.bfloat16)
    return one_hot.reshape(voxels.shape[0], 64 * levels_count)


def group_cells(rows_in, samples, grid_x, grid_y, grid_z):
    channels = rows_in.shape[1]
    blocks = rows_in.reshape(samples, grid_x // 2, 2, grid_y // 2, 2, grid_z // 2, 2, channels)
    blocks = blocks.transpose(0, 1, 3, 5, 2, 4, 6, 7)
    return blocks.reshape(-1, 8 * channels)


def spread_cells(rows_in, samples, grid_x, grid_y, grid_z):
    channels = rows_in.shape[1] // 8
    blocks = rows_in.reshape(samples, grid_x // 2, grid_y // 2, grid_z // 2, 2, 2, 2, channels)
    blocks = blocks.transpose(0, 1, 4, 2, 5, 3, 6, 7)
    return blocks.reshape(-1, channels)


def encode(facies, w_embed, w_conv, w_head):
    samples = facies.shape[0]
    grid_x, grid_y, grid_z = PATCH_X // 4, PATCH_Y // 4, PATCH_Z // 4
    one_hot = embed_rows(facies, w_embed.shape[0] // 64)
    pre_embed = jnp.dot(one_hot, w_embed, preferred_element_type=jnp.float32)
    hidden = jax.nn.silu(pre_embed).astype(jnp.bfloat16)
    conv_in = group_cells(hidden, samples, grid_x, grid_y, grid_z)
    pre_conv = jnp.dot(conv_in, w_conv, preferred_element_type=jnp.float32)
    pooled = jnp.mean(jax.nn.silu(pre_conv).reshape(samples, -1, pre_conv.shape[1]), axis=1).astype(jnp.bfloat16)
    latent = jnp.dot(pooled, w_head, preferred_element_type=jnp.float32).astype(jnp.bfloat16)
    return one_hot, pre_embed, conv_in, pre_conv, pooled, latent


def kernel_block(queries, query_square, key_rows, latent_width):
    inner_prod = lax.dot_general(queries, key_rows, (((1,), (1,)), ((), ())), preferred_element_type=jnp.float32)
    key_float = key_rows.astype(jnp.float32)
    key_square = jnp.sum(key_float * key_float, axis=1)
    square_dist = query_square[:, None] + key_square[None, :] - 2.0 * inner_prod
    kernel = jnp.exp(-square_dist / latent_width)
    mixed = jnp.dot(kernel.astype(jnp.bfloat16), key_rows, preferred_element_type=jnp.float32)
    return jnp.sum(kernel, axis=1), mixed


def back_signals(grid_dims, cotangent, pre_embed, pre_conv, w_conv, w_head):
    samples = cotangent.shape[0]
    cell_count = pre_conv.shape[0] // samples
    back_pool = lax.dot_general(cotangent, w_head, (((1,), (1,)), ((), ())), preferred_element_type=jnp.float32)
    slope = silu_slope(pre_conv).reshape(samples, cell_count, pre_conv.shape[1])
    conv_grad = ((back_pool[:, None, :] / cell_count) * slope).reshape(pre_conv.shape).astype(jnp.bfloat16)
    back_rows = lax.dot_general(conv_grad, w_conv, (((1,), (1,)), ((), ())), preferred_element_type=jnp.float32)
    spread = spread_cells(back_rows, samples, grid_dims[0], grid_dims[1], grid_dims[2])
    embed_grad = (spread * silu_slope(pre_embed)).astype(jnp.bfloat16)
    return conv_grad, embed_grad


def inner_rows(left_rows, right_rows):
    return lax.dot_general(left_rows, right_rows, (((0,), (0,)), ((), ())), preferred_element_type=jnp.float32)


def block_grads(facies_block, cotangent, w_embed, w_conv, w_head):
    one_hot, pre_embed, conv_in, pre_conv, pooled, latent = encode(facies_block, w_embed, w_conv, w_head)
    grid_dims = (PATCH_X // 4, PATCH_Y // 4, PATCH_Z // 4)
    conv_grad, embed_grad = back_signals(grid_dims, cotangent, pre_embed, pre_conv, w_conv, w_head)
    return inner_rows(one_hot, embed_grad), inner_rows(conv_in, conv_grad), inner_rows(pooled, cotangent)


def reference(facies, prior_draws, recon_grad, w_embed, w_conv, w_head):
    block_count = SAMPLES // SAMP_DEV
    facies_blocks = facies.reshape((block_count, SAMP_DEV) + facies.shape[1:])

    def latent_block(facies_block):
        return encode(facies_block, w_embed, w_conv, w_head)[5]

    latents = lax.map(latent_block, facies_blocks).reshape(SAMPLES, LAT)
    query_float = latents.astype(jnp.float32)
    query_square = jnp.sum(query_float * query_float, axis=1)
    self_sum, self_mix = kernel_block(latents, query_square, latents, LAT)
    cross_sum, cross_mix = kernel_block(latents, query_square, prior_draws, LAT)
    pull = (-32.0 / SAMPLES) * ((self_sum - cross_sum)[:, None] * query_float - self_mix + cross_mix)
    cotangent = (recon_grad.astype(jnp.float32) + pull).astype(jnp.bfloat16)
    cotan_blocks = cotangent.reshape(block_count, SAMP_DEV, LAT)

    def backward_pass(totals, inputs):
        terms = block_grads(inputs[0], inputs[1], w_embed, w_conv, w_head)
        return (totals[0] + terms[0], totals[1] + terms[1], totals[2] + terms[2]), None

    zero_grads = (jnp.zeros(w_embed.shape, jnp.float32), jnp.zeros(w_conv.shape, jnp.float32), jnp.zeros(w_head.shape, jnp.float32))
    summed = lax.scan(backward_pass, zero_grads, (facies_blocks, cotan_blocks))[0]
    return summed[0], summed[1], summed[2]
```

```python
import functools

import jax
import jax.numpy as jnp
import numpy as np
from jax import lax
from jax.experimental import pallas as pl
from jax.experimental.pallas import tpu as pltpu
from jax.sharding import PartitionSpec as P

MESH = pl.DeviceIdType.MESH
F32 = jnp.float32
BF16 = jnp.bfloat16
CELLS = 256.0


def lane_regroup():
    table = np.zeros((512, 1024), np.float32)
    for dx in range(4):
        for dy in range(4):
            for c in range(8):
                for dz in range(4):
                    for copy in range(2):
                        table[dx * 128 + dy * 32 + c * 4 + dz, c * 128 + copy * 64 + dx * 16 + dy * 4 + dz] = 1
    return table


def dot(left, right, dims=((1,), (0,))):
    return lax.dot_general(left, right, (dims, ((), ())), preferred_element_type=F32)


def step_kernel(
    dp_size, fsdp_size, reduce_embed,
    fac, prior, recon, w_embed, w_conv, w_head, regroup,
    out_embed, out_conv, out_head,
    w_float, w_perm, one_hot, pre_embed, hidden, pre_conv, conv_grad, embed_grad,
    fac_lanes, stage, early, pooled, cotan, head_full,
    gc, c1, c2, c3, cfin, ge, e1, e2, e3, efin, embed_local,
    early_send, early_recv, pool_send, pool_recv,
    s1_send, s1_recv, s2_send, s2_recv, s3_send, s3_recv, ag_send, ag_recv, fac_sem,
):
    n = dp_size * fsdp_size
    xs = dp_size // 2
    my_dp = lax.axis_index("dp")
    my_f = lax.axis_index("fsdp")
    me = my_dp * fsdp_size + my_f
    core = lax.rem(my_dp, 2)
    my_x = my_dp // 2

    def peer(i):
        flat = lax.rem(me + i, n)
        return {"dp": flat // fsdp_size, "fsdp": lax.rem(flat, fsdp_size)}

    def fac_copy(b):
        return pltpu.make_async_copy(fac.at[:, :, b * 128 : (b + 1) * 128], fac_lanes.at[b], fac_sem.at[b])

    for b in list(range(0, 16, 2)) + list(range(1, 16, 2)):
        fac_copy(b).start()

    barrier = pltpu.get_barrier_semaphore()

    def greet(i, carry):
        pl.semaphore_signal(barrier, inc=1, device_id=peer(i), device_id_type=MESH)
        return carry

    lax.fori_loop(1, n, greet, 0)

    for k, ref in enumerate((prior, recon)):
        rows = ref[...].astype(F32)
        for q in range(4):
            stage[k * 16 + q * 4 : k * 16 + q * 4 + 4, :] = rows[:, q * 128 : (q + 1) * 128]
    early[me] = stage[...].astype(BF16)

    w_float[...] = w_embed[...].astype(F32)
    for k in range(4):
        w_perm[k * 64 : (k + 1) * 64, :] = w_float[pl.ds(k, 64, stride=4), :].astype(BF16)

    lane = lax.broadcasted_iota(jnp.int32, (256, 1024), 1)
    low_level = ((lane // 64) % 2).astype(F32)
    for q in (0, 2, 1, 3):
        dxa, db = q // 2, q % 2
        if dxa == 0:
            for b2 in range(8):
                fac_copy(2 * b2 + db).wait()
        tiles = []
        for s in range(4):
            for b2 in range(8):
                b = 2 * b2 + db
                tiles.append(
                    jnp.concatenate(
                        [
                            fac_lanes[b, s, pl.ds(4 * dxa + dx, 8, stride=8), :]
                            for dx in range(4)
                        ],
                        axis=1,
                    )
                )
        values = jnp.concatenate(tiles, axis=0).astype(F32).astype(BF16)
        levels = dot(values, regroup[...])
        low = (levels == low_level).astype(F32).astype(BF16)
        high = (levels == low_level + 2.0).astype(F32).astype(BF16)
        for c in range(8):
            one_hot[q, :, c * 256 : c * 256 + 128] = low[:, c * 128 : (c + 1) * 128]
            one_hot[q, :, c * 256 + 128 : (c + 1) * 256] = high[:, c * 128 : (c + 1) * 128]
        for c in range(8):
            pre = dot(one_hot[q, :, c * 256 : (c + 1) * 256], w_perm[...])
            pre_embed[q, :, c * 128 : (c + 1) * 128] = pre
            hidden[q, :, c * 128 : (c + 1) * 128] = (pre / (1.0 + jnp.exp(-pre))).astype(BF16)

    pl.semaphore_wait(barrier, n - 1)

    def early_copy(i):
        return pltpu.make_async_remote_copy(
            src_ref=early.at[me], dst_ref=early.at[me],
            send_sem=early_send.at[i], recv_sem=early_recv.at[me],
            device_id=peer(i), device_id_type=MESH,
        )

    def pool_copy(i):
        return pltpu.make_async_remote_copy(
            src_ref=pooled.at[me], dst_ref=pooled.at[me],
            send_sem=pool_send.at[i], recv_sem=pool_recv.at[me],
            device_id=peer(i), device_id_type=MESH,
        )

    def arrived(buffer, send, recv, i):
        slot = lax.rem(me + i, n)
        return pltpu.make_async_remote_copy(
            src_ref=buffer.at[slot], dst_ref=buffer.at[slot],
            send_sem=send.at[i], recv_sem=recv.at[slot],
            device_id=peer(i), device_id_type=MESH,
        )

    def start_early(i, carry):
        early_copy(i).start()
        return carry

    lax.fori_loop(1, n, start_early, 0)

    sums = [jnp.zeros((1, 256), F32) for _ in range(4)]
    for c2i in range(4):
        total = None
        for q in range(4):
            term = dot(hidden[q, :, c2i * 256 : (c2i + 1) * 256], w_conv[q * 256 : (q + 1) * 256, :])
            total = term if total is None else total + term
        pre_conv[c2i] = total
        act = total / (1.0 + jnp.exp(-total))
        for s in range(4):
            sums[s] = sums[s] + jnp.sum(act[s * 64 : (s + 1) * 64], axis=0, keepdims=True)
    for s in range(4):
        mean = (sums[s] / CELLS).astype(BF16).astype(F32)
        for half in range(2):
            pooled[me, half * 4 + s : half * 4 + s + 1, :] = mean[:, half * 128 : (half + 1) * 128]

    def start_pool(i, carry):
        pool_copy(i).start()
        return carry

    lax.fori_loop(1, n, start_pool, 0)

    for q in range(4):
        for c in range(8):
            pre = pre_embed[q, :, c * 128 : (c + 1) * 128]
            gate = 1.0 / (1.0 + jnp.exp(-pre))
            pre_embed[q, :, c * 128 : (c + 1) * 128] = gate * (1.0 + pre * (1.0 - gate))
    for c2i in range(4):
        pre = pre_conv[c2i]
        gate = 1.0 / (1.0 + jnp.exp(-pre))
        pre_conv[c2i] = gate * (1.0 + pre * (1.0 - gate))

    def wait_rows(i, carry):
        arrived(early, early_send, early_recv, i).wait_recv()
        arrived(pooled, pool_send, pool_recv, i).wait_recv()
        return carry

    lax.fori_loop(1, n, wait_rows, 0)

    rows8 = 8 * n
    used_row = (lax.broadcasted_iota(jnp.int32, (rows8, 1), 0) % 8) < 4
    used_col = (lax.broadcasted_iota(jnp.int32, (rows8, rows8), 1) % 8) < 4

    def lower(tile):
        return pltpu.roll(tile, rows8 - 4, 0)

    pool_flat = pooled[...].reshape(rows8, 128)
    pool_all = jnp.where(used_row, jnp.concatenate([pool_flat, lower(pool_flat)], axis=1), 0.0).astype(BF16)
    latent = dot(pool_all, w_head[...]).astype(BF16)
    latent_float = latent.astype(F32)

    def unfold(first):
        quarters = []
        for t in range(2):
            tile = early[:, first + 16 * 0 : first + 16, :].astype(F32)[:, 8 * t : 8 * t + 8, :].reshape(rows8, 128)
            quarters += [tile, lower(tile)]
        return jnp.where(used_row, jnp.concatenate(quarters, axis=1), 0.0)

    prior_float = unfold(0)
    recon_all = unfold(16)
    query_square = jnp.sum(latent_float * latent_float, axis=1, keepdims=True)

    def kernel_block(keys, keys_float):
        inner = dot(latent, keys, ((1,), (1,)))
        square = jnp.sum(keys_float * keys_float, axis=1, keepdims=True)
        square_row = jnp.transpose(jnp.broadcast_to(square, (rows8, rows8)))
        weight = jnp.exp(-(query_square + square_row - 2.0 * inner) / 512.0)
        weight = jnp.where(used_col, weight, 0.0)
        return jnp.sum(weight, axis=1, keepdims=True), dot(weight.astype(BF16), keys)

    self_sum, self_mix = kernel_block(latent, latent_float)
    cross_sum, cross_mix = kernel_block(prior_float.astype(BF16), prior_float)
    pull = (-32.0 / (4 * n)) * ((self_sum - cross_sum) * latent_float - self_mix + cross_mix)
    cot = jnp.where(used_row, recon_all + pull, 0.0).astype(BF16)
    cotan[...] = cot.astype(F32)
    mine = cotan[pl.ds(pl.multiple_of(me * 8, 8), 8), :].astype(BF16)
    back_pool = dot(mine, w_head[...], ((1,), (1,))) / CELLS

    for c2i in range(4):
        for s in range(4):
            grad = back_pool[s : s + 1, :] * pre_conv[c2i, s * 64 : (s + 1) * 64, :]
            conv_grad[c2i, s * 64 : (s + 1) * 64, :] = grad.astype(BF16)

    def at_dp(x, c):
        return {"dp": x * 2 + c, "fsdp": my_f}

    def chunk1(k, buf, land, x, f):
        slot = (k * xs + x) * fsdp_size + f
        return pltpu.make_async_remote_copy(
            src_ref=buf.at[1 - core, x, f], dst_ref=land.at[x, f],
            send_sem=s1_send.at[slot], recv_sem=s1_recv.at[slot],
            device_id=at_dp(my_x, 1 - core), device_id_type=MESH,
        )

    def chunk2(k, buf, land, i, f):
        other = lax.rem(my_x + i, xs)
        slot = (k * xs + i) * fsdp_size + f
        return pltpu.make_async_remote_copy(
            src_ref=buf.at[core, other, f], dst_ref=land.at[i, f],
            send_sem=s2_send.at[slot], recv_sem=s2_recv.at[slot],
            device_id=at_dp(other, core), device_id_type=MESH,
        )

    def chunk3(k, buf, land, i):
        other = lax.rem(my_f + i, fsdp_size)
        slot = k * fsdp_size + i
        return pltpu.make_async_remote_copy(
            src_ref=buf.at[core, my_x, other], dst_ref=land.at[i],
            send_sem=s3_send.at[slot], recv_sem=s3_recv.at[slot],
            device_id={"dp": my_dp, "fsdp": other}, device_id_type=MESH,
        )

    def gather(k, buf, i):
        other = lax.rem(my_dp + i, dp_size)
        slot = core * xs + my_x
        return pltpu.make_async_remote_copy(
            src_ref=buf.at[slot], dst_ref=buf.at[slot],
            send_sem=ag_send.at[k * dp_size + i], recv_sem=ag_recv.at[k * dp_size + i],
            device_id={"dp": other, "fsdp": my_f}, device_id_type=MESH,
        )

    def gathered(k, buf, i):
        other = lax.rem(my_dp + dp_size - i, dp_size)
        slot = lax.rem(other, 2) * xs + other // 2
        return pltpu.make_async_remote_copy(
            src_ref=buf.at[slot], dst_ref=buf.at[slot],
            send_sem=ag_send.at[k * dp_size + i], recv_sem=ag_recv.at[k * dp_size + i],
            device_id={"dp": other, "fsdp": my_f}, device_id_type=MESH,
        )

    order_x = [i for i in range(1, xs)] + [0]
    order_f = [i for i in range(1, fsdp_size)] + [0]

    def start_core(k, buf, land):
        for i in order_x:
            for j in order_f:
                chunk1(k, buf, land, lax.rem(my_x + i, xs), lax.rem(my_f + j, fsdp_size)).start()

    def pass_x(k, buf, land1, land2):
        for i in order_x:
            x = lax.rem(my_x + i, xs)
            for j in order_f:
                f = lax.rem(my_f + j, fsdp_size)
                chunk1(k, buf, land1, x, f).wait_recv()
                buf[core, x, f] = buf[core, x, f] + land1[x, f]
                if i:
                    chunk2(k, buf, land2, i, f).start()

    def pass_z(k, buf, land2, land3):
        for j in order_f:
            f = lax.rem(my_f + j, fsdp_size)
            total = buf[core, my_x, f]
            for i in range(1, xs):
                chunk2(k, buf, land2, i, f).wait_recv()
                total = total + land2[i, f]
            buf[core, my_x, f] = total
            if j:
                chunk3(k, buf, land3, j).start()

    def finish(k, buf, land3, final):
        total = buf[core, my_x, my_f]
        for j in range(1, fsdp_size):
            chunk3(k, buf, land3, j).wait_recv()
            total = total + land3[j]
        final[core * xs + my_x] = total
        for i in range(1, dp_size):
            gather(k, final, i).start()

    def collect(k, buf, land1, land2, land3, final, out):
        for i in range(1, dp_size):
            gathered(k, final, i).wait_recv()
        piece = final.shape[1]
        for slot in range(dp_size):
            out[slot * piece : (slot + 1) * piece, :] = final[slot]

    def drain(k, buf, land1, land2, land3, final):
        for i in range(xs):
            for f in range(fsdp_size):
                chunk1(k, buf, land1, i, f).wait_send()
                if i:
                    chunk2(k, buf, land2, i, f).wait_send()
        for j in range(1, fsdp_size):
            chunk3(k, buf, land3, j).wait_send()
        for i in range(1, dp_size):
            gather(k, final, i).wait_send()

    def place(buf, value, first):
        piece = buf.shape[3]
        for at in range(value.shape[0] // piece):
            number = first // piece + at
            f, rest = divmod(number, 2 * xs)
            c, x = divmod(rest, xs)
            buf[c, x, f] = value[at * piece : (at + 1) * piece, :]

    for q in range(4):
        total = None
        for c2i in range(4):
            term = dot(hidden[q, :, c2i * 256 : (c2i + 1) * 256], conv_grad[c2i], ((0,), (0,)))
            total = term if total is None else total + term
        place(gc, total, q * 256)
    start_core(0, gc, c1)

    head_full[...] = dot(pool_all, cot, ((0,), (0,)))
    head_rows = 256 // fsdp_size
    out_head[...] = head_full[pl.ds(pl.multiple_of(my_f * head_rows, 8), head_rows), :]

    def embed_block(q):
        for c2i in range(4):
            back = dot(conv_grad[c2i], w_conv[q * 256 : (q + 1) * 256, :], ((1,), (1,)))
            at = slice(c2i * 256, (c2i + 1) * 256)
            embed_grad[q, :, at] = (back * pre_embed[q, :, at]).astype(BF16)
        total = None
        for c in range(8):
            term = dot(
                embed_grad[q, :, c * 128 : (c + 1) * 128], one_hot[q, :, c * 256 : (c + 1) * 256], ((0,), (0,))
            )
            total = term if total is None else total + term
        return total

    acc = embed_block(0) + embed_block(1)
    pass_x(0, gc, c1, c2)
    acc = acc + embed_block(2) + embed_block(3)
    flipped = jnp.transpose(acc)
    for k in range(4):
        embed_local[pl.ds(k, 64, stride=4), :] = flipped[k * 64 : (k + 1) * 64, :]
    if reduce_embed:
        place(ge, embed_local[...], 0)
        start_core(1, ge, e1)
    pass_z(0, gc, c2, c3)
    if reduce_embed:
        pass_x(1, ge, e1, e2)
        pass_z(1, ge, e2, e3)
    finish(0, gc, c3, cfin)
    if reduce_embed:
        finish(1, ge, e3, efin)
    collect(0, gc, c1, c2, c3, cfin, out_conv)
    if reduce_embed:
        collect(1, ge, e1, e2, e3, efin, out_embed)
    else:
        out_embed[...] = embed_local[...]

    drain(0, gc, c1, c2, c3, cfin)
    if reduce_embed:
        drain(1, ge, e1, e2, e3, efin)

    def wait_sent(i, carry):
        early_copy(i).wait_send()
        pool_copy(i).wait_send()
        return carry

    lax.fori_loop(1, n, wait_sent, 0)


def shards(dp_size, fsdp_size, facies, prior_draws, recon_grad, w_embed, w_conv, w_head):
    n = dp_size * fsdp_size
    xs = dp_size // 2
    conv_piece = 1024 // (fsdp_size * dp_size)
    embed_piece = 256 // (fsdp_size * dp_size)
    reduce_embed = embed_piece % 8 == 0
    embed_slot = embed_piece if reduce_embed else 8
    regroup = jnp.asarray(lane_regroup(), BF16)
    vm = pltpu.VMEM
    dma = pltpu.SemaphoreType.DMA

    def reduction(piece, width):
        return [
            vm((2, xs, fsdp_size, piece, width), F32),
            vm((xs, fsdp_size, piece, width), F32),
            vm((xs, fsdp_size, piece, width), F32),
            vm((fsdp_size, piece, width), F32),
            vm((dp_size, piece, width), F32),
        ]

    embed_rows = 256 // fsdp_size if reduce_embed else 256
    out = pl.pallas_call(
        functools.partial(step_kernel, dp_size, fsdp_size, reduce_embed),
        out_shape=(
            jax.ShapeDtypeStruct((embed_rows, 128), F32),
            jax.ShapeDtypeStruct((1024 // fsdp_size, 256), F32),
            jax.ShapeDtypeStruct((256 // fsdp_size, 512), F32),
        ),
        in_specs=[pl.BlockSpec(memory_space=pl.ANY)] + [pl.BlockSpec(memory_space=pltpu.VMEM)] * 6,
        out_specs=(pl.BlockSpec(memory_space=pltpu.VMEM),) * 3,
        scratch_shapes=[
            vm((256, 128), F32),
            vm((256, 128), BF16),
            vm((4, 256, 2048), BF16),
            vm((4, 256, 1024), F32),
            vm((4, 256, 1024), BF16),
            vm((4, 256, 256), F32),
            vm((4, 256, 256), BF16),
            vm((4, 256, 1024), BF16),
            vm((16, 4, 64, 128), jnp.int32),
            vm((32, 128), F32),
            vm((n, 32, 128), BF16),
            vm((n, 8, 128), F32),
            vm((8 * n, 512), F32),
            vm((256, 512), F32),
            *reduction(conv_piece, 256),
            *reduction(embed_slot, 128),
            vm((256, 128), F32),
            dma((n,)), dma((n,)), dma((n,)), dma((n,)),
            dma((2 * xs * fsdp_size,)), dma((2 * xs * fsdp_size,)),
            dma((2 * xs * fsdp_size,)), dma((2 * xs * fsdp_size,)),
            dma((2 * fsdp_size,)), dma((2 * fsdp_size,)),
            dma((2 * dp_size,)), dma((2 * dp_size,)), dma((16,)),
        ],
        compiler_params=pltpu.CompilerParams(
            collective_id=0, has_side_effects=True, vmem_limit_bytes=56 * 1024 * 1024
        ),
        name="encoder_step",
    )(facies, prior_draws, recon_grad, w_embed, w_conv, w_head, regroup)
    if reduce_embed:
        return out
    share = lax.psum_scatter(out[0], "fsdp", scatter_dimension=0, tiled=True)
    return (lax.psum(share, "dp"), out[1], out[2])


def solution(mesh):
    return jax.shard_map(
        functools.partial(shards, mesh.shape["dp"], mesh.shape["fsdp"]),
        mesh=mesh,
        in_specs=(
            P(("groups", "dp", "fsdp"), None, None),
            P(("groups", "dp", "fsdp"), None),
            P(("groups", "dp", "fsdp"), None),
            P(),
            P(),
            P(),
        ),
        out_specs=(
            P(("groups", "fsdp"), None),
            P(("groups", "fsdp"), None),
            P(("groups", "fsdp"), None),
        ),
        check_vma=False,
    )
```

```python
import functools

import jax
import jax.numpy as jnp
import numpy as np
from jax import lax
from jax.experimental import pallas as pl
from jax.experimental.pallas import tpu as pltpu
from jax.sharding import PartitionSpec as P

MESH = pl.DeviceIdType.MESH
F32 = jnp.float32
BF16 = jnp.bfloat16
CELLS = 256.0


def lane_regroup():
    table = np.zeros((512, 1024), np.float32)
    for dx in range(4):
        for dy in range(4):
            for c in range(8):
                for dz in range(4):
                    for copy in range(2):
                        table[dx * 128 + dy * 32 + c * 4 + dz, c * 128 + copy * 64 + dx * 16 + dy * 4 + dz] = 1
    return table


def dot(left, right, dims=((1,), (0,))):
    return lax.dot_general(left, right, (dims, ((), ())), preferred_element_type=F32)


def sigmoid(v):
    return 0.5 + 0.5 * jnp.tanh(0.5 * v)


def step_kernel(
    dp_size, fsdp_size, reduce_embed,
    fac, prior, recon, w_embed, w_conv_hbm, w_head_hbm, regroup_hbm,
    out_embed, out_conv, out_head,
    w_float, w_perm, one_hot, pre_embed, hidden, pre_conv, conv_grad, embed_grad,
    w_conv, w_head, regroup, fac_lanes, stage, pool_stage, early, pooled, cotan, head_full,
    gc, c1, c2, c3, cfin, ge, e1, e2, e3, efin, embed_local,
    early_send, early_recv, pool_send, pool_recv,
    s1_send, s1_recv, s2_send, s2_recv, s3_send, s3_recv, ag_send, ag_recv, fac_sem, weight_sem, out_sem,
):
    n = dp_size * fsdp_size
    xs = dp_size // 2
    my_dp = lax.axis_index("dp")
    my_f = lax.axis_index("fsdp")
    me = my_dp * fsdp_size + my_f
    core = lax.rem(my_dp, 2)
    my_x = my_dp // 2

    def peer(i):
        flat = lax.rem(me + i, n)
        return {"dp": flat // fsdp_size, "fsdp": lax.rem(flat, fsdp_size)}

    def fac_copy(b):
        return pltpu.make_async_copy(fac.at[:, :, b * 128 : (b + 1) * 128], fac_lanes.at[b], fac_sem.at[b])

    weight_copies = [
        pltpu.make_async_copy(src, dst, weight_sem.at[i])
        for i, (src, dst) in enumerate(((regroup_hbm, regroup), (w_conv_hbm, w_conv), (w_head_hbm, w_head)))
    ]
    for b in range(0, 16, 2):
        fac_copy(b).start()
    weight_copies[0].start()
    for b in range(1, 16, 2):
        fac_copy(b).start()
    weight_copies[1].start()
    weight_copies[2].start()

    barrier = pltpu.get_barrier_semaphore()

    def greet(i, carry):
        pl.semaphore_signal(barrier, inc=1, device_id=peer(i), device_id_type=MESH)
        return carry

    lax.fori_loop(1, n, greet, 0)

    for k, ref in enumerate((prior, recon)):
        rows = ref[...].astype(F32)
        for q in range(4):
            stage[k * 16 + q * 4 : k * 16 + q * 4 + 4, :] = rows[:, q * 128 : (q + 1) * 128]
    early[me] = stage[...].astype(BF16)

    w_float[...] = w_embed[...].astype(F32)
    for k in range(4):
        w_perm[k * 64 : (k + 1) * 64, :] = w_float[pl.ds(k, 64, stride=4), :].astype(BF16)

    def early_copy(i):
        return pltpu.make_async_remote_copy(
            src_ref=early.at[me], dst_ref=early.at[me],
            send_sem=early_send.at[i], recv_sem=early_recv.at[me],
            device_id=peer(i), device_id_type=MESH,
        )

    def pool_copy(i):
        return pltpu.make_async_remote_copy(
            src_ref=pooled.at[me], dst_ref=pooled.at[me],
            send_sem=pool_send.at[i], recv_sem=pool_recv.at[me],
            device_id=peer(i), device_id_type=MESH,
        )

    def arrived(buffer, send, recv, i):
        slot = lax.rem(me + i, n)
        return pltpu.make_async_remote_copy(
            src_ref=buffer.at[slot], dst_ref=buffer.at[slot],
            send_sem=send.at[i], recv_sem=recv.at[slot],
            device_id=peer(i), device_id_type=MESH,
        )

    def start_early(i, carry):
        early_copy(i).start()
        return carry

    lane = lax.broadcasted_iota(jnp.int32, (256, 1024), 1)
    low_level = ((lane // 64) % 2).astype(F32)
    for q in (0, 2, 1, 3):
        dxa, db = q // 2, q % 2
        if dxa == 0:
            for b2 in range(8):
                fac_copy(2 * b2 + db).wait()
        tiles = []
        for s in range(4):
            for b2 in range(8):
                b = 2 * b2 + db
                tiles.append(
                    jnp.concatenate(
                        [
                            fac_lanes[b, s, pl.ds(4 * dxa + dx, 8, stride=8), :]
                            for dx in range(4)
                        ],
                        axis=1,
                    )
                )
        if q == 0:
            weight_copies[0].wait()
        values = jnp.concatenate(tiles, axis=0).astype(F32).astype(BF16)
        levels = dot(values, regroup[...])
        low = (levels == low_level).astype(F32).astype(BF16)
        high = (levels == low_level + 2.0).astype(F32).astype(BF16)
        for c in range(8):
            one_hot[q, :, c * 256 : c * 256 + 128] = low[:, c * 128 : (c + 1) * 128]
            one_hot[q, :, c * 256 + 128 : (c + 1) * 256] = high[:, c * 128 : (c + 1) * 128]
        for c in range(8):
            pre = dot(one_hot[q, :, c * 256 : (c + 1) * 256], w_perm[...])
            pre_embed[q, :, c * 128 : (c + 1) * 128] = pre
            hidden[q, :, c * 128 : (c + 1) * 128] = (pre * sigmoid(pre)).astype(BF16)
        if q == 0:
            pl.semaphore_wait(barrier, n - 1)
            lax.fori_loop(1, n, start_early, 0)

    weight_copies[1].wait()
    weight_copies[2].wait()
    sums = [jnp.zeros((1, 256), F32) for _ in range(4)]
    for c2i in range(4):
        total = None
        for q in range(4):
            term = dot(hidden[q, :, c2i * 256 : (c2i + 1) * 256], w_conv[q * 256 : (q + 1) * 256, :])
            total = term if total is None else total + term
        pre_conv[c2i] = total
        act = total * sigmoid(total)
        for s in range(4):
            sums[s] = sums[s] + jnp.sum(act[s * 64 : (s + 1) * 64], axis=0, keepdims=True)
    for s in range(4):
        mean = (sums[s] / CELLS).astype(BF16).astype(F32)
        for half in range(2):
            pool_stage[half * 4 + s : half * 4 + s + 1, :] = mean[:, half * 128 : (half + 1) * 128]
    pooled[me] = pool_stage[...].astype(BF16)

    def start_pool(i, carry):
        pool_copy(i).start()
        return carry

    lax.fori_loop(1, n, start_pool, 0)

    for q in range(4):
        for c in range(8):
            pre = pre_embed[q, :, c * 128 : (c + 1) * 128]
            gate = sigmoid(pre)
            pre_embed[q, :, c * 128 : (c + 1) * 128] = gate * (1.0 + pre * (1.0 - gate))
    for c2i in range(4):
        pre = pre_conv[c2i]
        gate = sigmoid(pre)
        pre_conv[c2i] = gate * (1.0 + pre * (1.0 - gate))

    def wait_rows(i, carry):
        arrived(early, early_send, early_recv, i).wait_recv()
        arrived(pooled, pool_send, pool_recv, i).wait_recv()
        return carry

    lax.fori_loop(1, n, wait_rows, 0)

    rows8 = 8 * n
    used_row = (lax.broadcasted_iota(jnp.int32, (rows8, 1), 0) % 8) < 4
    used_col = (lax.broadcasted_iota(jnp.int32, (rows8, rows8), 1) % 8) < 4

    def lower(tile):
        return pltpu.roll(tile, rows8 - 4, 0)

    pool_flat = pooled[...].astype(F32).reshape(rows8, 128)
    pool_all = jnp.where(used_row, jnp.concatenate([pool_flat, lower(pool_flat)], axis=1), 0.0).astype(BF16)
    latent = dot(pool_all, w_head[...]).astype(BF16)
    latent_float = latent.astype(F32)

    def unfold(first):
        quarters = []
        for t in range(2):
            tile = early[:, first + 16 * 0 : first + 16, :].astype(F32)[:, 8 * t : 8 * t + 8, :].reshape(rows8, 128)
            quarters += [tile, lower(tile)]
        return jnp.where(used_row, jnp.concatenate(quarters, axis=1), 0.0)

    prior_float = unfold(0)
    recon_all = unfold(16)
    query_square = jnp.sum(latent_float * latent_float, axis=1, keepdims=True)

    def kernel_block(keys, keys_float):
        inner = dot(latent, keys, ((1,), (1,)))
        square = jnp.sum(keys_float * keys_float, axis=1, keepdims=True)
        square_row = jnp.transpose(jnp.broadcast_to(square, (rows8, rows8)))
        weight = jnp.exp(-(query_square + square_row - 2.0 * inner) / 512.0)
        weight = jnp.where(used_col, weight, 0.0)
        return jnp.sum(weight, axis=1, keepdims=True), dot(weight.astype(BF16), keys)

    self_sum, self_mix = kernel_block(latent, latent_float)
    cross_sum, cross_mix = kernel_block(prior_float.astype(BF16), prior_float)
    pull = (-32.0 / (4 * n)) * ((self_sum - cross_sum) * latent_float - self_mix + cross_mix)
    cot = jnp.where(used_row, recon_all + pull, 0.0).astype(BF16)
    cotan[...] = cot.astype(F32)
    mine = cotan[pl.ds(pl.multiple_of(me * 8, 8), 8), :].astype(BF16)
    back_pool = dot(mine, w_head[...], ((1,), (1,))) / CELLS

    for c2i in range(4):
        for s in range(4):
            grad = back_pool[s : s + 1, :] * pre_conv[c2i, s * 64 : (s + 1) * 64, :]
            conv_grad[c2i, s * 64 : (s + 1) * 64, :] = grad.astype(BF16)

    def at_dp(x, c):
        return {"dp": x * 2 + c, "fsdp": my_f}

    def chunk1(k, buf, land, x, f):
        slot = (k * xs + x) * fsdp_size + f
        return pltpu.make_async_remote_copy(
            src_ref=buf.at[1 - core, x, f], dst_ref=land.at[x, f],
            send_sem=s1_send.at[slot], recv_sem=s1_recv.at[slot],
            device_id=at_dp(my_x, 1 - core), device_id_type=MESH,
        )

    def chunk2(k, buf, land, i, f):
        other = lax.rem(my_x + i, xs)
        slot = (k * xs + i) * fsdp_size + f
        return pltpu.make_async_remote_copy(
            src_ref=buf.at[core, other, f], dst_ref=land.at[i, f],
            send_sem=s2_send.at[slot], recv_sem=s2_recv.at[slot],
            device_id=at_dp(other, core), device_id_type=MESH,
        )

    def chunk3(k, buf, land, i):
        other = lax.rem(my_f + i, fsdp_size)
        slot = k * fsdp_size + i
        return pltpu.make_async_remote_copy(
            src_ref=buf.at[core, my_x, other], dst_ref=land.at[i],
            send_sem=s3_send.at[slot], recv_sem=s3_recv.at[slot],
            device_id={"dp": my_dp, "fsdp": other}, device_id_type=MESH,
        )

    def gather(k, buf, i):
        other = lax.rem(my_dp + i, dp_size)
        slot = core * xs + my_x
        return pltpu.make_async_remote_copy(
            src_ref=buf.at[slot], dst_ref=buf.at[slot],
            send_sem=ag_send.at[k * dp_size + i], recv_sem=ag_recv.at[k * dp_size + i],
            device_id={"dp": other, "fsdp": my_f}, device_id_type=MESH,
        )

    def gathered(k, buf, i):
        other = lax.rem(my_dp + dp_size - i, dp_size)
        slot = lax.rem(other, 2) * xs + other // 2
        return pltpu.make_async_remote_copy(
            src_ref=buf.at[slot], dst_ref=buf.at[slot],
            send_sem=ag_send.at[k * dp_size + i], recv_sem=ag_recv.at[k * dp_size + i],
            device_id={"dp": other, "fsdp": my_f}, device_id_type=MESH,
        )

    order_x = [i for i in range(1, xs)] + [0]
    order_f = [i for i in range(1, fsdp_size)] + [0]

    def send_core(k, buf, land, i, j):
        chunk1(k, buf, land, lax.rem(my_x + i, xs), lax.rem(my_f + j, fsdp_size)).start()

    def start_core(k, buf, land):
        for i in order_x:
            for j in order_f:
                send_core(k, buf, land, i, j)

    def pass_x(k, buf, land1, land2, i, j):
        x = lax.rem(my_x + i, xs)
        f = lax.rem(my_f + j, fsdp_size)
        chunk1(k, buf, land1, x, f).wait_recv()
        buf[core, x, f] = buf[core, x, f] + land1[x, f]
        if i:
            chunk2(k, buf, land2, i, f).start()

    def pass_z(k, buf, land2, land3, j):
        f = lax.rem(my_f + j, fsdp_size)
        total = buf[core, my_x, f]
        for i in range(1, xs):
            chunk2(k, buf, land2, i, f).wait_recv()
            total = total + land2[i, f]
        buf[core, my_x, f] = total
        if j:
            chunk3(k, buf, land3, j).start()

    def finish(k, buf, land3, final):
        total = buf[core, my_x, my_f]
        for j in range(1, fsdp_size):
            chunk3(k, buf, land3, j).wait_recv()
            total = total + land3[j]
        final[core * xs + my_x] = total
        for i in range(1, dp_size):
            gather(k, final, i).start()

    def out_copy(k, final, out, slot):
        piece = final.shape[1]
        rows = pl.ds(pl.multiple_of(slot * piece, 8), piece)
        return pltpu.make_async_copy(final.at[slot], out.at[rows, :], out_sem.at[k, slot])

    def collect(k, final, out):
        out_copy(k, final, out, core * xs + my_x).start()
        for i in range(1, dp_size):
            other = lax.rem(my_dp + dp_size - i, dp_size)
            gathered(k, final, i).wait_recv()
            out_copy(k, final, out, lax.rem(other, 2) * xs + other // 2).start()

    def collected(k, final, out):
        for slot in range(dp_size):
            out_copy(k, final, out, slot).wait()

    def drain(k, buf, land1, land2, land3, final):
        for i in range(xs):
            for f in range(fsdp_size):
                chunk1(k, buf, land1, i, f).wait_send()
                if i:
                    chunk2(k, buf, land2, i, f).wait_send()
        for j in range(1, fsdp_size):
            chunk3(k, buf, land3, j).wait_send()
        for i in range(1, dp_size):
            gather(k, final, i).wait_send()

    def place(buf, value, block, per_block):
        piece = buf.shape[3]
        for at in range(value.shape[0] // piece):
            f, rest = divmod(at, 2 * xs)
            c, x = divmod(rest, xs)
            buf[c, x, block * per_block + f] = value[at * piece : (at + 1) * piece, :]

    rotated = fsdp_size == 4
    for j in (1, 2, 3, 0):
        q = lax.rem(my_f + j, 4) if rotated else j
        total = None
        for c2i in range(4):
            term = dot(hidden[q, :, c2i * 256 : (c2i + 1) * 256], conv_grad[c2i], ((0,), (0,)))
            total = term if total is None else total + term
        place(gc, total, q, fsdp_size // 4)
        if rotated:
            for i in order_x[:-1]:
                send_core(0, gc, c1, i, j)
    if rotated:
        for j in order_f:
            send_core(0, gc, c1, 0, j)
    else:
        start_core(0, gc, c1)

    head_full[...] = dot(pool_all, cot, ((0,), (0,)))
    head_rows = 256 // fsdp_size
    head_copy = pltpu.make_async_copy(
        head_full.at[pl.ds(pl.multiple_of(my_f * head_rows, 8), head_rows), :], out_head, out_sem.at[2, 0]
    )
    head_copy.start()

    def embed_block(q):
        for c2i in range(4):
            back = dot(conv_grad[c2i], w_conv[q * 256 : (q + 1) * 256, :], ((1,), (1,)))
            at = slice(c2i * 256, (c2i + 1) * 256)
            embed_grad[q, :, at] = (back * pre_embed[q, :, at]).astype(BF16)
        total = None
        for c in range(8):
            term = dot(
                embed_grad[q, :, c * 128 : (c + 1) * 128], one_hot[q, :, c * 256 : (c + 1) * 256], ((0,), (0,))
            )
            total = term if total is None else total + term
        return total

    acc = embed_block(0)
    for i in order_x[:-1]:
        for j in order_f:
            pass_x(0, gc, c1, c2, i, j)
    acc = acc + embed_block(1)
    for j in order_f:
        pass_x(0, gc, c1, c2, 0, j)
    acc = acc + embed_block(2)
    pass_z(0, gc, c2, c3, order_f[0])
    acc = acc + embed_block(3)
    flipped = jnp.transpose(acc)
    for k in range(4):
        embed_local[pl.ds(k, 64, stride=4), :] = flipped[k * 64 : (k + 1) * 64, :]
    if reduce_embed:
        place(ge, embed_local[...], 0, 0)
        start_core(1, ge, e1)
    for j in order_f[1:2]:
        pass_z(0, gc, c2, c3, j)
    if reduce_embed:
        for i in order_x:
            for j in order_f:
                pass_x(1, ge, e1, e2, i, j)
    for j in order_f[2:]:
        pass_z(0, gc, c2, c3, j)
    if reduce_embed:
        for j in order_f:
            pass_z(1, ge, e2, e3, j)
    finish(0, gc, c3, cfin)
    if reduce_embed:
        finish(1, ge, e3, efin)
    collect(0, cfin, out_conv)
    if reduce_embed:
        collect(1, efin, out_embed)
        collected(1, efin, out_embed)
    else:
        local_copy = pltpu.make_async_copy(embed_local, out_embed, out_sem.at[1, 0])
        local_copy.start()
        local_copy.wait()
    collected(0, cfin, out_conv)
    head_copy.wait()

    drain(0, gc, c1, c2, c3, cfin)
    if reduce_embed:
        drain(1, ge, e1, e2, e3, efin)

    def wait_sent(i, carry):
        early_copy(i).wait_send()
        pool_copy(i).wait_send()
        return carry

    lax.fori_loop(1, n, wait_sent, 0)


def copy_kernel(a_in, b_in, c_in, a_out, b_out, c_out, sem):
    copies = [
        pltpu.make_async_copy(src, dst, sem.at[i])
        for i, (src, dst) in enumerate(((a_in, a_out), (b_in, b_out), (c_in, c_out)))
    ]
    for copy in copies:
        copy.start()
    for copy in copies:
        copy.wait()


def copied(arrays):
    anywhere = pl.BlockSpec(memory_space=pl.ANY)
    return pl.pallas_call(
        copy_kernel,
        out_shape=tuple(jax.ShapeDtypeStruct(a.shape, a.dtype) for a in arrays),
        in_specs=[anywhere] * 3,
        out_specs=(anywhere,) * 3,
        scratch_shapes=[pltpu.SemaphoreType.DMA((3,))],
        name="outputs",
    )(*arrays)


def shards(dp_size, fsdp_size, facies, prior_draws, recon_grad, w_embed, w_conv, w_head):
    n = dp_size * fsdp_size
    xs = dp_size // 2
    conv_piece = 1024 // (fsdp_size * dp_size)
    embed_piece = 256 // (fsdp_size * dp_size)
    reduce_embed = embed_piece % 8 == 0
    embed_slot = embed_piece if reduce_embed else 8
    regroup = jnp.asarray(lane_regroup(), BF16)
    vm = pltpu.VMEM
    dma = pltpu.SemaphoreType.DMA

    def reduction(piece, width):
        return [
            vm((2, xs, fsdp_size, piece, width), F32),
            vm((xs, fsdp_size, piece, width), F32),
            vm((xs, fsdp_size, piece, width), F32),
            vm((fsdp_size, piece, width), F32),
            vm((dp_size, piece, width), F32),
        ]

    embed_rows = 256 // fsdp_size if reduce_embed else 256
    out = pl.pallas_call(
        functools.partial(step_kernel, dp_size, fsdp_size, reduce_embed),
        out_shape=(
            jax.ShapeDtypeStruct((embed_rows, 128), F32),
            jax.ShapeDtypeStruct((1024 // fsdp_size, 256), F32),
            jax.ShapeDtypeStruct((256 // fsdp_size, 512), F32),
        ),
        in_specs=[
            pl.BlockSpec(memory_space=space) for space in (pl.ANY, vm, vm, vm, pl.ANY, pl.ANY, pl.ANY)
        ],
        out_specs=(pl.BlockSpec(memory_space=pl.ANY),) * 3,
        scratch_shapes=[
            vm((256, 128), F32),
            vm((256, 128), BF16),
            vm((4, 256, 2048), BF16),
            vm((4, 256, 1024), F32),
            vm((4, 256, 1024), BF16),
            vm((4, 256, 256), F32),
            vm((4, 256, 256), BF16),
            vm((4, 256, 1024), BF16),
            vm((1024, 256), BF16),
            vm((256, 512), BF16),
            vm((512, 1024), BF16),
            vm((16, 4, 64, 128), jnp.int32),
            vm((32, 128), F32),
            vm((8, 128), F32),
            vm((n, 32, 128), BF16),
            vm((n, 8, 128), BF16),
            vm((8 * n, 512), F32),
            vm((256, 512), F32),
            *reduction(conv_piece, 256),
            *reduction(embed_slot, 128),
            vm((256, 128), F32),
            dma((n,)), dma((n,)), dma((n,)), dma((n,)),
            dma((2 * xs * fsdp_size,)), dma((2 * xs * fsdp_size,)),
            dma((2 * xs * fsdp_size,)), dma((2 * xs * fsdp_size,)),
            dma((2 * fsdp_size,)), dma((2 * fsdp_size,)),
            dma((2 * dp_size,)), dma((2 * dp_size,)), dma((16,)), dma((3,)), dma((3, dp_size)),
        ],
        compiler_params=pltpu.CompilerParams(
            collective_id=0, has_side_effects=True, vmem_limit_bytes=56 * 1024 * 1024
        ),
        name="encoder_step",
    )(facies, prior_draws, recon_grad, w_embed, w_conv, w_head, regroup)
    if reduce_embed:
        return copied(out)
    share = lax.psum_scatter(out[0], "fsdp", scatter_dimension=0, tiled=True)
    return (lax.psum(share, "dp"), out[1], out[2])


def solution(mesh):
    return jax.shard_map(
        functools.partial(shards, mesh.shape["dp"], mesh.shape["fsdp"]),
        mesh=mesh,
        in_specs=(
            P(("groups", "dp", "fsdp"), None, None),
            P(("groups", "dp", "fsdp"), None),
            P(("groups", "dp", "fsdp"), None),
            P(),
            P(),
            P(),
        ),
        out_specs=(
            P(("groups", "fsdp"), None),
            P(("groups", "fsdp"), None),
            P(("groups", "fsdp"), None),
        ),
        check_vma=False,
    )
```

```python
import functools

import jax
import jax.numpy as jnp
import numpy as np
from jax import lax
from jax.experimental import pallas as pl
from jax.experimental.pallas import tpu as pltpu
from jax.sharding import PartitionSpec as P

MESH = pl.DeviceIdType.MESH
F32 = jnp.float32
BF16 = jnp.bfloat16
CELLS = 256.0


def lane_regroup():
    table = np.zeros((512, 1024), np.float32)
    for dx in range(4):
        for dy in range(4):
            for c in range(8):
                for dz in range(4):
                    for copy in range(2):
                        table[dx * 128 + dy * 32 + c * 4 + dz, c * 128 + copy * 64 + dx * 16 + dy * 4 + dz] = 1
    return table


def dot(left, right, dims=((1,), (0,))):
    return lax.dot_general(left, right, (dims, ((), ())), preferred_element_type=F32)


def sigmoid(v):
    return 0.5 + 0.5 * jnp.tanh(0.5 * v)


def step_kernel(
    dp_size, fsdp_size, reduce_embed,
    fac, prior, recon, w_embed, w_conv_hbm, w_head_hbm, regroup_hbm,
    out_embed, out_conv, out_head,
    w_float, w_perm, one_hot, pre_embed, hidden, pre_conv, conv_grad, embed_grad,
    w_conv, w_head, regroup, fac_lanes, stage, pool_stage, early, pooled, cotan, head_full,
    gc, c1, c2, c3, cfin, ge, e1, e2, e3, efin, embed_local,
    early_send, early_recv, pool_send, pool_recv,
    s1_send, s1_recv, s2_send, s2_recv, s3_send, s3_recv, ag_send, ag_recv, fac_sem, weight_sem, out_sem,
):
    n = dp_size * fsdp_size
    xs = dp_size // 2
    my_dp = lax.axis_index("dp")
    my_f = lax.axis_index("fsdp")
    me = my_dp * fsdp_size + my_f
    core = lax.rem(my_dp, 2)
    my_x = my_dp // 2

    def peer(i):
        flat = lax.rem(me + i, n)
        return {"dp": flat // fsdp_size, "fsdp": lax.rem(flat, fsdp_size)}

    def fac_copy(b):
        return pltpu.make_async_copy(fac.at[:, :, b * 128 : (b + 1) * 128], fac_lanes.at[b], fac_sem.at[b])

    weight_copies = [
        pltpu.make_async_copy(src, dst, weight_sem.at[i])
        for i, (src, dst) in enumerate(((regroup_hbm, regroup), (w_conv_hbm, w_conv), (w_head_hbm, w_head)))
    ]
    for b in range(0, 16, 2):
        fac_copy(b).start()
    weight_copies[0].start()
    for b in range(1, 16, 2):
        fac_copy(b).start()
    weight_copies[1].start()
    weight_copies[2].start()

    barrier = pltpu.get_barrier_semaphore()

    def greet(i, carry):
        pl.semaphore_signal(barrier, inc=1, device_id=peer(i), device_id_type=MESH)
        return carry

    lax.fori_loop(1, n, greet, 0)

    for k, ref in enumerate((prior, recon)):
        rows = ref[...].astype(F32)
        for q in range(4):
            stage[k * 16 + q * 4 : k * 16 + q * 4 + 4, :] = rows[:, q * 128 : (q + 1) * 128]
    early[me] = stage[...].astype(BF16)

    w_float[...] = w_embed[...].astype(F32)
    for k in range(4):
        w_perm[k * 64 : (k + 1) * 64, :] = w_float[pl.ds(k, 64, stride=4), :].astype(BF16)

    def early_copy(i):
        return pltpu.make_async_remote_copy(
            src_ref=early.at[me], dst_ref=early.at[me],
            send_sem=early_send.at[i], recv_sem=early_recv.at[me],
            device_id=peer(i), device_id_type=MESH,
        )

    def pool_copy(i):
        return pltpu.make_async_remote_copy(
            src_ref=pooled.at[me], dst_ref=pooled.at[me],
            send_sem=pool_send.at[i], recv_sem=pool_recv.at[me],
            device_id=peer(i), device_id_type=MESH,
        )

    def arrived(buffer, send, recv, i):
        slot = lax.rem(me + i, n)
        return pltpu.make_async_remote_copy(
            src_ref=buffer.at[slot], dst_ref=buffer.at[slot],
            send_sem=send.at[i], recv_sem=recv.at[slot],
            device_id=peer(i), device_id_type=MESH,
        )

    def start_early(i, carry):
        early_copy(i).start()
        return carry

    lane = lax.broadcasted_iota(jnp.int32, (256, 1024), 1)
    low_level = ((lane // 64) % 2).astype(F32)
    for q in (0, 2, 1, 3):
        dxa, db = q // 2, q % 2
        if dxa == 0:
            for b2 in range(8):
                fac_copy(2 * b2 + db).wait()
        tiles = []
        for s in range(4):
            for b2 in range(8):
                b = 2 * b2 + db
                tiles.append(
                    jnp.concatenate(
                        [
                            fac_lanes[b, s, pl.ds(4 * dxa + dx, 8, stride=8), :]
                            for dx in range(4)
                        ],
                        axis=1,
                    )
                )
        if q == 0:
            weight_copies[0].wait()
        values = jnp.concatenate(tiles, axis=0).astype(F32).astype(BF16)
        levels = dot(values, regroup[...])
        low = (levels == low_level).astype(F32).astype(BF16)
        high = (levels == low_level + 2.0).astype(F32).astype(BF16)
        for c in range(8):
            one_hot[q, :, c * 256 : c * 256 + 128] = low[:, c * 128 : (c + 1) * 128]
            one_hot[q, :, c * 256 + 128 : (c + 1) * 256] = high[:, c * 128 : (c + 1) * 128]
        for c in range(8):
            pre = dot(one_hot[q, :, c * 256 : (c + 1) * 256], w_perm[...])
            pre_embed[q, :, c * 128 : (c + 1) * 128] = pre
            hidden[q, :, c * 128 : (c + 1) * 128] = (pre * sigmoid(pre)).astype(BF16)
        if q == 0:
            pl.semaphore_wait(barrier, n - 1)
            lax.fori_loop(1, n, start_early, 0)

    weight_copies[1].wait()
    weight_copies[2].wait()
    sums = [jnp.zeros((1, 256), F32) for _ in range(4)]
    for c2i in range(4):
        total = None
        for q in range(4):
            term = dot(hidden[q, :, c2i * 256 : (c2i + 1) * 256], w_conv[q * 256 : (q + 1) * 256, :])
            total = term if total is None else total + term
        pre_conv[c2i] = total
        act = total * sigmoid(total)
        for s in range(4):
            sums[s] = sums[s] + jnp.sum(act[s * 64 : (s + 1) * 64], axis=0, keepdims=True)
    for s in range(4):
        mean = (sums[s] / CELLS).astype(BF16).astype(F32)
        for half in range(2):
            pool_stage[half * 4 + s : half * 4 + s + 1, :] = mean[:, half * 128 : (half + 1) * 128]
    pooled[me] = pool_stage[...].astype(BF16)

    def start_pool(i, carry):
        pool_copy(i).start()
        return carry

    lax.fori_loop(1, n, start_pool, 0)

    for q in range(4):
        for c in range(8):
            pre = pre_embed[q, :, c * 128 : (c + 1) * 128]
            gate = sigmoid(pre)
            pre_embed[q, :, c * 128 : (c + 1) * 128] = gate * (1.0 + pre * (1.0 - gate))
    for c2i in range(4):
        pre = pre_conv[c2i]
        gate = sigmoid(pre)
        pre_conv[c2i] = gate * (1.0 + pre * (1.0 - gate))

    def wait_rows(i, carry):
        arrived(early, early_send, early_recv, i).wait_recv()
        arrived(pooled, pool_send, pool_recv, i).wait_recv()
        return carry

    lax.fori_loop(1, n, wait_rows, 0)

    rows8 = 8 * n
    used_row = (lax.broadcasted_iota(jnp.int32, (rows8, 1), 0) % 8) < 4
    used_col = (lax.broadcasted_iota(jnp.int32, (rows8, rows8), 1) % 8) < 4

    def lower(tile):
        return pltpu.roll(tile, rows8 - 4, 0)

    pool_flat = pooled[...].astype(F32).reshape(rows8, 128)
    pool_all = jnp.where(used_row, jnp.concatenate([pool_flat, lower(pool_flat)], axis=1), 0.0).astype(BF16)
    latent = dot(pool_all, w_head[...]).astype(BF16)
    latent_float = latent.astype(F32)

    def unfold(first):
        quarters = []
        for t in range(2):
            tile = early[:, first + 16 * 0 : first + 16, :].astype(F32)[:, 8 * t : 8 * t + 8, :].reshape(rows8, 128)
            quarters += [tile, lower(tile)]
        return jnp.where(used_row, jnp.concatenate(quarters, axis=1), 0.0)

    prior_float = unfold(0)
    recon_all = unfold(16)
    query_square = jnp.sum(latent_float * latent_float, axis=1, keepdims=True)

    def kernel_block(keys, keys_float):
        inner = dot(latent, keys, ((1,), (1,)))
        square = jnp.sum(keys_float * keys_float, axis=1, keepdims=True)
        square_row = jnp.transpose(jnp.broadcast_to(square, (rows8, rows8)))
        weight = jnp.exp(-(query_square + square_row - 2.0 * inner) / 512.0)
        weight = jnp.where(used_col, weight, 0.0)
        return jnp.sum(weight, axis=1, keepdims=True), dot(weight.astype(BF16), keys)

    self_sum, self_mix = kernel_block(latent, latent_float)
    cross_sum, cross_mix = kernel_block(prior_float.astype(BF16), prior_float)
    pull = (-32.0 / (4 * n)) * ((self_sum - cross_sum) * latent_float - self_mix + cross_mix)
    cot = jnp.where(used_row, recon_all + pull, 0.0).astype(BF16)
    cotan[...] = cot.astype(F32)
    mine = cotan[pl.ds(pl.multiple_of(me * 8, 8), 8), :].astype(BF16)
    back_pool = dot(mine, w_head[...], ((1,), (1,))) / CELLS

    for c2i in range(4):
        for s in range(4):
            grad = back_pool[s : s + 1, :] * pre_conv[c2i, s * 64 : (s + 1) * 64, :]
            conv_grad[c2i, s * 64 : (s + 1) * 64, :] = grad.astype(BF16)

    def at_dp(x, c):
        return {"dp": x * 2 + c, "fsdp": my_f}

    def chunk1(k, buf, land, x, f):
        slot = (k * xs + x) * fsdp_size + f
        return pltpu.make_async_remote_copy(
            src_ref=buf.at[1 - core, x, f], dst_ref=land.at[x, f],
            send_sem=s1_send.at[slot], recv_sem=s1_recv.at[slot],
            device_id=at_dp(my_x, 1 - core), device_id_type=MESH,
        )

    def chunk2(k, buf, land, i, f):
        other = lax.rem(my_x + i, xs)
        slot = (k * xs + i) * fsdp_size + f
        return pltpu.make_async_remote_copy(
            src_ref=buf.at[core, other, f], dst_ref=land.at[i, f],
            send_sem=s2_send.at[slot], recv_sem=s2_recv.at[slot],
            device_id=at_dp(other, core), device_id_type=MESH,
        )

    def chunk3(k, buf, land, i):
        other = lax.rem(my_f + i, fsdp_size)
        slot = k * fsdp_size + i
        return pltpu.make_async_remote_copy(
            src_ref=buf.at[core, my_x, other], dst_ref=land.at[i],
            send_sem=s3_send.at[slot], recv_sem=s3_recv.at[slot],
            device_id={"dp": my_dp, "fsdp": other}, device_id_type=MESH,
        )

    def gather(k, buf, i):
        other = lax.rem(my_dp + i, dp_size)
        slot = core * xs + my_x
        return pltpu.make_async_remote_copy(
            src_ref=buf.at[slot], dst_ref=buf.at[slot],
            send_sem=ag_send.at[k * dp_size + i], recv_sem=ag_recv.at[k * dp_size + i],
            device_id={"dp": other, "fsdp": my_f}, device_id_type=MESH,
        )

    def gathered(k, buf, i):
        other = lax.rem(my_dp + dp_size - i, dp_size)
        slot = lax.rem(other, 2) * xs + other // 2
        return pltpu.make_async_remote_copy(
            src_ref=buf.at[slot], dst_ref=buf.at[slot],
            send_sem=ag_send.at[k * dp_size + i], recv_sem=ag_recv.at[k * dp_size + i],
            device_id={"dp": other, "fsdp": my_f}, device_id_type=MESH,
        )

    order_x = [i for i in range(1, xs)] + [0]
    order_f = [i for i in range(1, fsdp_size)] + [0]

    def send_core(k, buf, land, i, j):
        chunk1(k, buf, land, lax.rem(my_x + i, xs), lax.rem(my_f + j, fsdp_size)).start()

    def start_core(k, buf, land):
        for i in order_x:
            for j in order_f:
                send_core(k, buf, land, i, j)

    def pass_x(k, buf, land1, land2, i, j):
        x = lax.rem(my_x + i, xs)
        f = lax.rem(my_f + j, fsdp_size)
        chunk1(k, buf, land1, x, f).wait_recv()
        buf[core, x, f] = buf[core, x, f] + land1[x, f]
        if i:
            chunk2(k, buf, land2, i, f).start()

    def pass_z(k, buf, land2, land3, j):
        f = lax.rem(my_f + j, fsdp_size)
        total = buf[core, my_x, f]
        for i in range(1, xs):
            chunk2(k, buf, land2, i, f).wait_recv()
            total = total + land2[i, f]
        buf[core, my_x, f] = total
        if j:
            chunk3(k, buf, land3, j).start()

    def finish(k, buf, land3, final):
        total = buf[core, my_x, my_f]
        for j in range(1, fsdp_size):
            chunk3(k, buf, land3, j).wait_recv()
            total = total + land3[j]
        final[core * xs + my_x] = total
        for i in range(1, dp_size):
            gather(k, final, i).start()

    def out_copy(k, final, out, slot):
        piece = final.shape[1]
        rows = pl.ds(pl.multiple_of(slot * piece, 8), piece)
        return pltpu.make_async_copy(final.at[slot], out.at[rows, :], out_sem.at[k, slot])

    def collect(k, final, out):
        out_copy(k, final, out, core * xs + my_x).start()
        for i in range(1, dp_size):
            other = lax.rem(my_dp + dp_size - i, dp_size)
            gathered(k, final, i).wait_recv()
            out_copy(k, final, out, lax.rem(other, 2) * xs + other // 2).start()

    def collected(k, final, out):
        for slot in range(dp_size):
            out_copy(k, final, out, slot).wait()

    def drain(k, buf, land1, land2, land3, final):
        for i in range(xs):
            for f in range(fsdp_size):
                chunk1(k, buf, land1, i, f).wait_send()
                if i:
                    chunk2(k, buf, land2, i, f).wait_send()
        for j in range(1, fsdp_size):
            chunk3(k, buf, land3, j).wait_send()
        for i in range(1, dp_size):
            gather(k, final, i).wait_send()

    def place(buf, value, block, per_block):
        piece = buf.shape[3]
        for at in range(value.shape[0] // piece):
            f, rest = divmod(at, 2 * xs)
            c, x = divmod(rest, xs)
            buf[c, x, block * per_block + f] = value[at * piece : (at + 1) * piece, :]

    rotated = fsdp_size == 4
    for j in (1, 2, 3, 0):
        q = lax.rem(my_f + j, 4) if rotated else j
        total = None
        for c2i in range(4):
            term = dot(hidden[q, :, c2i * 256 : (c2i + 1) * 256], conv_grad[c2i], ((0,), (0,)))
            total = term if total is None else total + term
        place(gc, total, q, fsdp_size // 4)
        if rotated:
            for i in order_x[:-1]:
                send_core(0, gc, c1, i, j)
    if rotated:
        for j in order_f:
            send_core(0, gc, c1, 0, j)
    else:
        start_core(0, gc, c1)

    head_full[...] = dot(pool_all, cot, ((0,), (0,)))
    head_rows = 256 // fsdp_size
    head_copy = pltpu.make_async_copy(
        head_full.at[pl.ds(pl.multiple_of(my_f * head_rows, 8), head_rows), :], out_head, out_sem.at[2, 0]
    )
    head_copy.start()

    def embed_block(q):
        for c2i in range(4):
            back = dot(conv_grad[c2i], w_conv[q * 256 : (q + 1) * 256, :], ((1,), (1,)))
            at = slice(c2i * 256, (c2i + 1) * 256)
            embed_grad[q, :, at] = (back * pre_embed[q, :, at]).astype(BF16)
        total = None
        for c in range(8):
            term = dot(
                embed_grad[q, :, c * 128 : (c + 1) * 128], one_hot[q, :, c * 256 : (c + 1) * 256], ((0,), (0,))
            )
            total = term if total is None else total + term
        return total

    acc = embed_block(0)
    for i in order_x[:-1]:
        for j in order_f:
            pass_x(0, gc, c1, c2, i, j)
    acc = acc + embed_block(1)
    for j in order_f:
        pass_x(0, gc, c1, c2, 0, j)
    acc = acc + embed_block(2)
    pass_z(0, gc, c2, c3, order_f[0])
    acc = acc + embed_block(3)
    flipped = jnp.transpose(acc)
    for k in range(4):
        embed_local[pl.ds(k, 64, stride=4), :] = flipped[k * 64 : (k + 1) * 64, :]
    if reduce_embed:
        place(ge, embed_local[...], 0, 0)
        start_core(1, ge, e1)
    for j in order_f[1:2]:
        pass_z(0, gc, c2, c3, j)
    if reduce_embed:
        for i in order_x:
            for j in order_f:
                pass_x(1, ge, e1, e2, i, j)
    for j in order_f[2:]:
        pass_z(0, gc, c2, c3, j)
    if reduce_embed:
        for j in order_f:
            pass_z(1, ge, e2, e3, j)
    finish(0, gc, c3, cfin)
    if reduce_embed:
        finish(1, ge, e3, efin)
    collect(0, cfin, out_conv)
    if reduce_embed:
        collect(1, efin, out_embed)
        collected(1, efin, out_embed)
    else:
        local_copy = pltpu.make_async_copy(embed_local, out_embed, out_sem.at[1, 0])
        local_copy.start()
        local_copy.wait()
    collected(0, cfin, out_conv)
    head_copy.wait()

    drain(0, gc, c1, c2, c3, cfin)
    if reduce_embed:
        drain(1, ge, e1, e2, e3, efin)

    def wait_sent(i, carry):
        early_copy(i).wait_send()
        pool_copy(i).wait_send()
        return carry

    lax.fori_loop(1, n, wait_sent, 0)


def copy_kernel(a_in, b_in, c_in, a_out, b_out, c_out):
    a_out[...] = a_in[...]
    b_out[...] = b_in[...]
    c_out[...] = c_in[...]


def copied(arrays):
    whole = pl.BlockSpec(memory_space=pltpu.VMEM)
    return pl.pallas_call(
        copy_kernel,
        out_shape=tuple(jax.ShapeDtypeStruct(a.shape, a.dtype) for a in arrays),
        in_specs=[whole] * 3,
        out_specs=(whole,) * 3,
        name="outputs",
    )(*arrays)


def shards(dp_size, fsdp_size, facies, prior_draws, recon_grad, w_embed, w_conv, w_head):
    n = dp_size * fsdp_size
    xs = dp_size // 2
    conv_piece = 1024 // (fsdp_size * dp_size)
    embed_piece = 256 // (fsdp_size * dp_size)
    reduce_embed = embed_piece % 8 == 0
    embed_slot = embed_piece if reduce_embed else 8
    regroup = jnp.asarray(lane_regroup(), BF16)
    vm = pltpu.VMEM
    dma = pltpu.SemaphoreType.DMA

    def reduction(piece, width):
        return [
            vm((2, xs, fsdp_size, piece, width), F32),
            vm((xs, fsdp_size, piece, width), F32),
            vm((xs, fsdp_size, piece, width), F32),
            vm((fsdp_size, piece, width), F32),
            vm((dp_size, piece, width), F32),
        ]

    embed_rows = 256 // fsdp_size if reduce_embed else 256
    out = pl.pallas_call(
        functools.partial(step_kernel, dp_size, fsdp_size, reduce_embed),
        out_shape=(
            jax.ShapeDtypeStruct((embed_rows, 128), F32),
            jax.ShapeDtypeStruct((1024 // fsdp_size, 256), F32),
            jax.ShapeDtypeStruct((256 // fsdp_size, 512), F32),
        ),
        in_specs=[
            pl.BlockSpec(memory_space=space) for space in (pl.ANY, vm, vm, vm, pl.ANY, pl.ANY, pl.ANY)
        ],
        out_specs=(pl.BlockSpec(memory_space=pl.ANY),) * 3,
        scratch_shapes=[
            vm((256, 128), F32),
            vm((256, 128), BF16),
            vm((4, 256, 2048), BF16),
            vm((4, 256, 1024), F32),
            vm((4, 256, 1024), BF16),
            vm((4, 256, 256), F32),
            vm((4, 256, 256), BF16),
            vm((4, 256, 1024), BF16),
            vm((1024, 256), BF16),
            vm((256, 512), BF16),
            vm((512, 1024), BF16),
            vm((16, 4, 64, 128), jnp.int32),
            vm((32, 128), F32),
            vm((8, 128), F32),
            vm((n, 32, 128), BF16),
            vm((n, 8, 128), BF16),
            vm((8 * n, 512), F32),
            vm((256, 512), F32),
            *reduction(conv_piece, 256),
            *reduction(embed_slot, 128),
            vm((256, 128), F32),
            dma((n,)), dma((n,)), dma((n,)), dma((n,)),
            dma((2 * xs * fsdp_size,)), dma((2 * xs * fsdp_size,)),
            dma((2 * xs * fsdp_size,)), dma((2 * xs * fsdp_size,)),
            dma((2 * fsdp_size,)), dma((2 * fsdp_size,)),
            dma((2 * dp_size,)), dma((2 * dp_size,)), dma((16,)), dma((3,)), dma((3, dp_size)),
        ],
        compiler_params=pltpu.CompilerParams(
            collective_id=0, has_side_effects=True, vmem_limit_bytes=56 * 1024 * 1024
        ),
        name="encoder_step",
    )(facies, prior_draws, recon_grad, w_embed, w_conv, w_head, regroup)
    if reduce_embed:
        return copied(out)
    share = lax.psum_scatter(out[0], "fsdp", scatter_dimension=0, tiled=True)
    return (lax.psum(share, "dp"), out[1], out[2])


def solution(mesh):
    return jax.shard_map(
        functools.partial(shards, mesh.shape["dp"], mesh.shape["fsdp"]),
        mesh=mesh,
        in_specs=(
            P(("groups", "dp", "fsdp"), None, None),
            P(("groups", "dp", "fsdp"), None),
            P(("groups", "dp", "fsdp"), None),
            P(),
            P(),
            P(),
        ),
        out_specs=(
            P(("groups", "fsdp"), None),
            P(("groups", "fsdp"), None),
            P(("groups", "fsdp"), None),
        ),
        check_vma=False,
    )
```
